32 devices in a mesh: grp: 1, seq: 32 (over z, y, x, core).
Axes of the slice: x: 2, y: 2, z: 4, core: 2. Of those that a mesh axis runs over, the one named last changes fastest.
Arguments:
- tokens: bfloat16 [4096, 4096], P(('grp', 'seq')), may hold values from -6 to 6
- gain: float32 [4096], replicated, may hold values from 0.5 to 6, as said below
- w_query: bfloat16 [4096, 2048], P('seq'), may hold values from -0.09375 to 0.09375
- key_value_weight: bfloat16 [4096, 1024], P('seq'), may hold values from -0.09375 to 0.09375
Outputs:
- attended: bfloat16 [4096, 2048], P(('grp', 'seq'))
The draws below stay inside these ranges and needn't reach their ends.
Inputs may be any that keep to these rules, and one draw needn't show every extreme that they name: gain is the same for all groups.
All inputs are finite; a program needn't handle non-finite values.
Results may differ from the reference program's by a relative error of at most 0.0055.
The reference program's roundings to bfloat16 on the way count: a program that leaves them out, or rounds other values in their place, can miss the bound.
Values may be sent and summed in bfloat16 or wider, within the bound.
No kernel may reach another device: no remote copies, remote signals or barrier semaphores. Data moves between devices by JAX's collectives and lax.ppermute only.
A program may use at most 128 MiB of HBM per device.

```python
import jax
import jax.numpy as jnp
from jax import lax

MODEL_WIDTH = 4096
HEAD_WIDTH = 128
HQ = 16
KEY_VALUE_HEADS = 4
QUERY_PER_KEY = 4
LOCAL_TOKENS = 128
SEQUENCE_TOKENS = 4096


def draw_gain(key, part):
    return jax.random.uniform(key, (MODEL_WIDTH,), jnp.float32, 0.5, 1.5)


def levels(rng, dims, split, smallest, high):
    factor_of, own = 1.0, jax.random.fold_in(rng, 6)
    for position, blocks in split:
        steps = jnp.exp(jax.random.uniform(jax.random.fold_in(own, position), (blocks,), jnp.float32, smallest / len(split), high / len(split)))
        factor_of = factor_of * jnp.repeat(steps, dims[position] // blocks).reshape([-1 if axis == position else 1 for axis in range(len(dims))])
    return factor_of


def noise(rng, extent, deviation, most, split=(), held_as=jnp.bfloat16):
    array = jax.random.normal(rng, extent, jnp.float32) * deviation
    if len(split) > 0:
        array = levels(rng, extent, split, -0.22, 0.18) * array
    return jnp.clip(array, min=-most, max=most).astype(held_as)


def setup_inputs(seed: int = 0, part: int = 0) -> dict:
    arg_keys = jax.random.split(jax.random.key(seed), 5)
    part_splits = jax.random.split(jax.random.fold_in(arg_keys[4], part), 5)
    tokens = noise(part_splits[0], (SEQUENCE_TOKENS, MODEL_WIDTH), 1.0, 6.0, ((0, 32),))
    gain = draw_gain(jax.random.fold_in(arg_keys[4], 71), part)
    w_query = noise(arg_keys[2], (MODEL_WIDTH, HQ * HEAD_WIDTH), MODEL_WIDTH ** -0.5, 0.09375, ((0, 32),))
    key_value_weight = noise(arg_keys[3], (MODEL_WIDTH, 2 * KEY_VALUE_HEADS * HEAD_WIDTH), MODEL_WIDTH ** -0.5, 0.09375, ((0, 32),))
    return dict(tokens=tokens, gain=gain, w_query=w_query, key_value_weight=key_value_weight)


ROPE_BASE = 500000.0

def apply_rotation(heads_in, token_positions):
    half_dim = HEAD_WIDTH // 2
    frequency = ROPE_BASE ** (-(jnp.arange(half_dim, dtype=jnp.float32) * 2.0 / HEAD_WIDTH))
    angles = token_positions.astype(jnp.float32)[:, None] * frequency[None, :]
    cosine = jnp.cos(angles)[:, None, :]
    sine_part = jnp.sin(angles)[:, None, :]
    first = heads_in[..., :half_dim]
    second = heads_in[..., half_dim:]
    return jnp.concatenate([first * cosine - second * sine_part, second * cosine + first * sine_part], axis=-1)

def reference(tokens, gain, w_query, key_value_weight):
    tok_float = tokens.astype(jnp.float32)
    mean_sq = lax.optimization_barrier(jnp.mean(tok_float * tok_float, axis=-1, keepdims=True))
    normed = (tok_float * lax.rsqrt(mean_sq + 1e-05) * gain[None, :]).astype(jnp.bfloat16)
    query_raw = jnp.dot(normed, w_query, preferred_element_type=jnp.float32)
    key_value_rows = jnp.dot(normed, key_value_weight, preferred_element_type=jnp.float32)
    token_positions = jnp.arange(SEQUENCE_TOKENS, dtype=jnp.int32)
    query_matrix = apply_rotation(query_raw.reshape(SEQUENCE_TOKENS, HQ, HEAD_WIDTH), token_positions).astype(jnp.bfloat16)
    query_matrix = query_matrix.reshape(SEQUENCE_TOKENS // LOCAL_TOKENS, LOCAL_TOKENS, KEY_VALUE_HEADS, QUERY_PER_KEY, HEAD_WIDTH)
    key_head_rows = apply_rotation(key_value_rows[:, :KEY_VALUE_HEADS * HEAD_WIDTH].reshape(SEQUENCE_TOKENS, KEY_VALUE_HEADS, HEAD_WIDTH), token_positions).astype(jnp.bfloat16)
    value_head_rows = key_value_rows[:, KEY_VALUE_HEADS * HEAD_WIDTH:].reshape(SEQUENCE_TOKENS, KEY_VALUE_HEADS, HEAD_WIDTH).astype(jnp.bfloat16)
    key_float = key_head_rows.astype(jnp.float32)
    value_float = value_head_rows.astype(jnp.float32)
    scale = 1.0 / HEAD_WIDTH ** 0.5
    starts = (jnp.arange(SEQUENCE_TOKENS // LOCAL_TOKENS, dtype=jnp.int32) * LOCAL_TOKENS).astype(jnp.int32)

    def one_block(inputs):
        query_block, first_row = inputs
        scores = jnp.einsum('qhgd,khd->qhgk', query_block.astype(jnp.float32), key_float) * scale
        query_pos = first_row + jnp.arange(LOCAL_TOKENS, dtype=jnp.int32)
        allowed = jnp.arange(SEQUENCE_TOKENS, dtype=jnp.int32)[None, :] <= query_pos[:, None]
        scores = jnp.where(allowed[:, None, None, :], scores, -1e+30)
        row_max = lax.optimization_barrier(jnp.max(scores, axis=-1, keepdims=True))
        expo = jnp.exp(scores - row_max)
        totals = lax.optimization_barrier(jnp.sum(expo, axis=-1))
        probs = expo.astype(jnp.bfloat16).astype(jnp.float32)
        weighted = jnp.einsum('qhgk,khd->qhgd', probs, value_float)
        result = weighted / totals[..., None]
        return result.reshape(LOCAL_TOKENS, HQ * HEAD_WIDTH).astype(jnp.bfloat16)
    attended = lax.map(one_block, (query_matrix, starts))
    return attended.reshape(SEQUENCE_TOKENS, HQ * HEAD_WIDTH)
```

```python
import math

import jax
import jax.numpy as jnp
from jax import lax
from jax.experimental import pallas as pl
from jax.experimental.pallas import tpu as pltpu
from jax.sharding import PartitionSpec as P

HEAD_WIDTH = 128
HQ = 16
ROPE_BASE = 500000.0
NEG = -1e30


def norm_kernel(order, j_shift, j_count, own_ref, tok_ref, gain_ref, out_ref):
    rows, width = tok_ref.shape
    tok = tok_ref[...].astype(jnp.float32)
    mean_sq = jnp.sum(tok * tok, axis=-1, keepdims=True) / width
    inv = lax.rsqrt(mean_sq + 1e-05)
    own = own_ref[0]
    base = own & ~((j_count - 1) << j_shift)
    block = width // (len(order) * j_count)
    place = 0
    for rel in order:
        for j in range(j_count):
            source = pl.multiple_of(((base ^ rel) | (j << j_shift)) * block, block)
            piece = tok_ref[:, pl.ds(source, block)].astype(jnp.float32)
            piece = piece * inv * gain_ref[:, pl.ds(source, block)]
            out_ref[:, place : place + block] = piece.astype(jnp.bfloat16)
            place += block


def normalize(tokens, gain, own, order, j_shift, j_count):
    def kernel(*refs):
        norm_kernel(order, j_shift, j_count, *refs)

    return pl.pallas_call(
        kernel,
        out_shape=jax.ShapeDtypeStruct(tokens.shape, jnp.bfloat16),
        in_specs=[
            pl.BlockSpec(memory_space=pltpu.SMEM),
            pl.BlockSpec(memory_space=pltpu.VMEM),
            pl.BlockSpec(memory_space=pltpu.VMEM),
        ],
        out_specs=pl.BlockSpec(memory_space=pltpu.VMEM),
        name="norm",
    )(own, tokens, gain.reshape(1, -1))


def attention(own, query, kv_near, kv_far, dims):
    rows, j_shift, j_count, group, bit_places = dims
    d = HEAD_WIDTH
    near_rows = kv_near.shape[0]
    slots = 2 * near_rows // rows
    per_tile = min(4, slots)
    tile = per_tile * rows
    height = group * rows
    factor = 1.0 / math.sqrt(d) * math.log2(math.e)

    def slot_of(block, own_id):
        rel = block ^ own_id
        place = (rel >> j_shift) & (j_count - 1)
        for bit, weight in bit_places:
            place = place + ((rel >> bit) & 1) * weight
        return place

    def kernel(own_ref, q_ref, near_ref, far_ref, out_ref, kv, scores, acc, sems):
        near = pltpu.make_async_copy(near_ref, kv.at[pl.ds(0, near_rows)], sems.at[0])
        far = pltpu.make_async_copy(far_ref, kv.at[pl.ds(near_rows, near_rows)], sems.at[1])
        near.start()
        far.start()
        near.wait()
        far.wait()
        own_id = own_ref[0]
        for b in range(j_count):
            block = own_id ^ (b << j_shift)
            tiles = block // per_tile + 1
            q = jnp.concatenate(
                [q_ref[b * rows : (b + 1) * rows, h * d : (h + 1) * d] for h in range(group)], axis=0
            )

            def starts(t):
                return [
                    pl.multiple_of(slot_of(t * per_tile + u, own_id) * rows, rows)
                    for u in range(per_tile)
                ]

            def score_tile(t):
                keys = jnp.concatenate([kv[pl.ds(s, rows), 0:d] for s in starts(t)], axis=0)
                return lax.dot_general(
                    q, keys, (((1,), (1,)), ((), ())), preferred_element_type=jnp.float32
                )

            def first_pass(t, top):
                s = score_tile(t)
                scores[t] = s
                for u in range(tile // 128):
                    top = jnp.maximum(top, s[:, u * 128 : (u + 1) * 128])
                return top

            top = lax.fori_loop(
                0, tiles - 1, first_pass, jnp.full((height, 128), NEG, jnp.float32)
            )
            last = tiles - 1
            s = score_tile(last)
            q_pos = block * rows + (
                lax.broadcasted_iota(jnp.int32, (height, tile), 0) & (rows - 1)
            )
            k_pos = last * tile + lax.broadcasted_iota(jnp.int32, (height, tile), 1)
            s = jnp.where(k_pos <= q_pos, s, NEG)
            scores[last] = s
            for u in range(tile // 128):
                top = jnp.maximum(top, s[:, u * 128 : (u + 1) * 128])
            peak = jnp.max(top, axis=-1, keepdims=True)
            acc[...] = jnp.zeros_like(acc)

            def second_pass(t, total):
                e = jnp.exp2((scores[t] - peak) * factor)
                for u in range(tile // 128):
                    total = total + e[:, u * 128 : (u + 1) * 128]
                vals = jnp.concatenate([kv[pl.ds(x, rows), d : 2 * d] for x in starts(t)], axis=0)
                acc[...] += jnp.dot(
                    e.astype(jnp.bfloat16), vals, preferred_element_type=jnp.float32
                )
                return total

            total = lax.fori_loop(0, tiles, second_pass, jnp.zeros((height, 128), jnp.float32))
            result = acc[...] / jnp.sum(total, axis=-1, keepdims=True)
            result = result.astype(jnp.bfloat16)
            owner = (block >> j_shift) & (j_count - 1)
            for h in range(group):
                out_ref[owner, :, h * d : (h + 1) * d] = result[h * rows : (h + 1) * rows]

    return pl.pallas_call(
        kernel,
        out_shape=jax.ShapeDtypeStruct((j_count, rows, group * d), jnp.bfloat16),
        in_specs=[
            pl.BlockSpec(memory_space=pltpu.SMEM),
            pl.BlockSpec(memory_space=pltpu.VMEM),
            pl.BlockSpec(memory_space=pl.ANY),
            pl.BlockSpec(memory_space=pl.ANY),
        ],
        out_specs=pl.BlockSpec(memory_space=pltpu.VMEM),
        scratch_shapes=[
            pltpu.VMEM((2 * near_rows, 2 * d), jnp.bfloat16),
            pltpu.VMEM((slots // per_tile, height, tile), jnp.float32),
            pltpu.VMEM((height, d), jnp.float32),
            pltpu.SemaphoreType.DMA((2,)),
        ],
        name="attention",
    )(own, query, kv_near, kv_far)


def build(count):
    bits = count.bit_length() - 1

    def on_device(tokens, gain, w_query, key_value_weight):
        rows = tokens.shape[0]
        d = HEAD_WIDTH
        kv_heads = key_value_weight.shape[1] // (2 * d)
        group = HQ // kv_heads
        j_shift, j_bits = 2, kv_heads.bit_length() - 1
        high = list(range(bits - 1, j_shift + j_bits - 1, -1))
        spread = high + [1, 0]
        own = lax.axis_index("seq")
        own_arr = own.astype(jnp.int32).reshape(1)

        def swap(value, mask):
            return lax.ppermute(value, "seq", [(s, s ^ mask) for s in range(count)])

        order = [0]
        for bit in spread:
            order = order + [o | (1 << bit) for o in order]
        bit_places = [(bit, kv_heads << n) for n, bit in enumerate(spread)]
        j_masks = [r << j_shift for r in range(kv_heads)]
        j_mask = j_masks[-1]
        groups = [[g | m for m in j_masks] for g in range(count) if g & j_mask == 0]

        def deal(value):
            return lax.all_to_all(value, "seq", 0, 0, axis_index_groups=groups)

        def by_head(w):
            return w.reshape(rows, kv_heads, -1).transpose(1, 0, 2)

        w_kv = jnp.concatenate(
            [by_head(key_value_weight[:, : kv_heads * d]), by_head(key_value_weight[:, kv_heads * d :])],
            axis=2,
        )
        w_all = deal(jnp.concatenate([w_kv, by_head(w_query)], axis=2))
        w_all = w_all.reshape(kv_heads * rows, -1)
        w_kv, w_q = w_all[:, : 2 * d], w_all[:, 2 * d :]

        def spread_rows(value):
            for bit in spread[:-1]:
                value = jnp.concatenate([value, swap(value, 1 << bit)], axis=0)
            return value, swap(value, 1 << spread[-1])

        normed = normalize(tokens, gain, own_arr, order, j_shift, kv_heads)
        blocks = [normed]
        for b in reversed(range(j_bits)):
            blocks = blocks + [swap(x, 1 << (j_shift + b)) for x in blocks]
        rel = [0]
        for b in reversed(range(j_bits)):
            rel = rel + [r | (1 << b) for r in rel]
        blocks = [blocks[rel.index(r)] for r in range(kv_heads)]
        normed_all = jnp.concatenate(blocks, axis=0)

        half_rows = tokens.shape[1] // 2

        def project(w):
            near, far = spread_rows(w)
            out = jnp.dot(normed_all[:, :half_rows], near, preferred_element_type=jnp.float32)
            return out + jnp.dot(
                normed_all[:, half_rows:], far, preferred_element_type=jnp.float32
            )

        half = d // 2
        frequency = ROPE_BASE ** (-(jnp.arange(half, dtype=jnp.float32) * 2.0 / d))
        ids = own ^ jnp.array(j_masks, jnp.int32)
        positions = (ids[:, None] * rows + jnp.arange(rows, dtype=jnp.int32)[None, :]).reshape(-1)
        angles = positions.astype(jnp.float32)[:, None] * frequency[None, :]
        cosine, sine = jnp.cos(angles), jnp.sin(angles)
        cosine = jnp.concatenate([cosine, cosine], axis=1)
        sine = jnp.concatenate([-sine, sine], axis=1)

        def rotate(u):
            return u * cosine + jnp.concatenate([u[:, half:], u[:, :half]], axis=1) * sine

        kv = project(w_kv)
        kv = jnp.concatenate([rotate(kv[:, :d]), kv[:, d:]], axis=1).astype(jnp.bfloat16)
        kv_near, kv_far = spread_rows(kv)
        q_raw = project(w_q)
        query = jnp.concatenate(
            [rotate(q_raw[:, h * d : (h + 1) * d]) for h in range(group)], axis=1
        ).astype(jnp.bfloat16)

        dims = (rows, j_shift, kv_heads, group, bit_places)
        out = deal(attention(own_arr, query, kv_near, kv_far, dims))
        return out.transpose(1, 0, 2).reshape(rows, HQ * d)

    return on_device


def solution(mesh):
    return jax.shard_map(
        build(mesh.shape["seq"]),
        mesh=mesh,
        in_specs=(P(("grp", "seq"), None), P(), P("seq", None), P("seq", None)),
        out_specs=P(("grp", "seq"), None),
        check_vma=False,
    )
```

```python
import math

import jax
import jax.numpy as jnp
from jax import lax
from jax.experimental import pallas as pl
from jax.experimental.pallas import tpu as pltpu
from jax.sharding import PartitionSpec as P


HEAD_WIDTH = 128
HQ = 16
ROPE_BASE = 500000.0
NEG = -1e30


def norm_kernel(order, j_shift, j_count, own_ref, tok_ref, gain_ref, *out_refs):
    _, width = tok_ref.shape
    tok = tok_ref[...].astype(jnp.float32)
    mean_sq = jnp.sum(tok * tok, axis=-1, keepdims=True) / width
    inv = lax.rsqrt(mean_sq + 1e-05)
    own = own_ref[0]
    base = own & ~((j_count - 1) << j_shift)
    block = width // (len(order) * j_count)
    places = [(rel, j) for rel in order for j in range(j_count)]
    for n, (rel, j) in enumerate(places):
        source = pl.multiple_of(((base ^ rel) | (j << j_shift)) * block, block)
        piece = tok_ref[:, pl.ds(source, block)].astype(jnp.float32)
        piece = piece * inv * gain_ref[:, pl.ds(source, block)]
        half, place = divmod(n * block, width // 2)
        out_refs[half][:, place : place + block] = piece.astype(jnp.bfloat16)


def normalize(tokens, gain, own, order, j_shift, j_count):
    def kernel(*refs):
        norm_kernel(order, j_shift, j_count, *refs)

    half = jax.ShapeDtypeStruct((tokens.shape[0], tokens.shape[1] // 2), jnp.bfloat16)
    return pl.pallas_call(
        kernel,
        out_shape=(half, half),
        in_specs=[
            pl.BlockSpec(memory_space=pltpu.SMEM),
            pl.BlockSpec(memory_space=pltpu.VMEM),
            pl.BlockSpec(memory_space=pltpu.VMEM),
        ],
        out_specs=(pl.BlockSpec(memory_space=pltpu.VMEM),) * 2,
        compiler_params=pltpu.CompilerParams(vmem_limit_bytes=4 << 20),
        name="norm",
    )(own, tokens, gain.reshape(1, -1))


def weights_by_head(w_query, key_value_weight, heads):
    rows, d = w_query.shape[0], HEAD_WIDTH
    wide = w_query.shape[1] // heads

    def kernel(q_ref, kv_ref, out_ref):
        for j in range(heads):
            out_ref[j, :, :d] = kv_ref[:, j * d : (j + 1) * d]
            out_ref[j, :, d : 2 * d] = kv_ref[:, (heads + j) * d : (heads + j + 1) * d]
            out_ref[j, :, 2 * d :] = q_ref[:, j * wide : (j + 1) * wide]

    return pl.pallas_call(
        kernel,
        out_shape=jax.ShapeDtypeStruct((heads, rows, 2 * d + wide), jnp.bfloat16),
        in_specs=[pl.BlockSpec(memory_space=pltpu.VMEM)] * 2,
        out_specs=pl.BlockSpec(memory_space=pltpu.VMEM),
        compiler_params=pltpu.CompilerParams(vmem_limit_bytes=4 << 20),
        name="weights",
    )(w_query, key_value_weight)


def attention(own, query, kv_parts, dims):
    rows, j_shift, j_count, group, bit_places = dims
    d = HEAD_WIDTH
    part_rows = kv_parts[0].shape[0]
    parts_n = len(kv_parts)
    slots = parts_n * part_rows // rows
    per_tile = 1 << j_shift
    tile = per_tile * rows
    height = group * rows
    factor = math.log2(math.e) / math.sqrt(d)
    sub = min(256, height)
    subs = height // sub
    chunks = tile // 128

    def slot_of(block, own_id):
        rel = block ^ own_id
        place = 0
        for bit, weight in bit_places:
            place = place + ((rel >> bit) & 1) * weight
        return place

    def kernel(own_ref, q_ref, *rest):
        part_refs, rest = rest[:parts_n], rest[parts_n:]
        out_ref, kv, sc0, sc1, top0, top1, tot_ref, acc, qs0, qs1, sems = rest
        scs, tops, qss = (sc0, sc1), (top0, top1), (qs0, qs1)
        copies = [
            pltpu.make_async_copy(ref, kv.at[pl.ds(n * part_rows, part_rows)], sems.at[n])
            for n, ref in enumerate(part_refs)
        ]
        for copy in copies:
            copy.start()
        own_id = own_ref[0]
        base = own_id & ~((j_count - 1) << j_shift)
        own_j = (own_id >> j_shift) & (j_count - 1)
        first_tile = base >> j_shift

        def starts(t):
            return [pl.multiple_of(slot_of(t * per_tile + u, own_id) * rows, rows) for u in range(per_tile)]

        def tile_of(t, col):
            return jnp.concatenate([kv[pl.ds(s, rows), col:col+d] for s in starts(t)], axis=0)

        def begin(k):
            place = pl.multiple_of((own_j ^ k) * rows, rows)
            for h in range(group):
                qss[k%2][h*rows:(h+1)*rows] = q_ref[pl.ds(place, rows), h * d : (h + 1) * d]
            tops[k%2][...] = jnp.full((height,128), NEG, jnp.float32)

        def first(k, t, keys, i, masked=False):
            r = slice(i*sub,(i+1)*sub)
            s = lax.dot_general(qss[k%2][r], keys, (((1,), (1,)), ((), ())), preferred_element_type=jnp.float32)
            if masked:
                block = base | (k << j_shift)
                q_pos = block * rows + ((i*sub + lax.broadcasted_iota(jnp.int32, (sub, tile), 0)) & (rows - 1))
                k_pos = t * tile + lax.broadcasted_iota(jnp.int32, (sub, tile), 1)
                s = jnp.where(k_pos <= q_pos, s, NEG)
            scs[k%2][t, r] = s
            top = tops[k%2][r]
            for u in range(chunks):
                top = jnp.maximum(top, s[:, u * 128 : (u + 1) * 128])
            tops[k%2][r] = top

        def second(k, t, vals, i):
            r = slice(i*sub,(i+1)*sub)
            peak = tops[k%2][r]
            total = tot_ref[r]
            parts = []
            for u in range(chunks):
                e = jnp.exp2((scs[k%2][t, r, u*128:(u+1)*128] - peak) * factor)
                total = total + e
                parts.append(e.astype(jnp.bfloat16))
            tot_ref[r] = total
            acc[r] += jnp.dot(jnp.concatenate(parts,axis=1), vals, preferred_element_type=jnp.float32)

        def loop(n, body):
            def step(t, c):
                body(t)
                return c

            lax.fori_loop(0, n, step, 0)

        def diag(k):
            t = first_tile + k
            keys = tile_of(t, 0)
            for i in range(subs):
                first(k, t, keys, i, True)
            for i in range(subs):
                r = slice(i*sub,(i+1)*sub)
                tops[k%2][r] = jnp.broadcast_to(jnp.max(tops[k%2][r], axis=-1, keepdims=True), (sub,128))

        def finish(k):
            for h in range(group):
                r=slice(h*rows,(h+1)*rows)
                result = (acc[r] / jnp.sum(tot_ref[r], axis=-1, keepdims=True)).astype(jnp.bfloat16)
                out_ref[k, :, h * d : (h + 1) * d] = result

        for copy in copies:
            copy.wait()
        begin(0)

        def head(t):
            keys = tile_of(t, 0)
            for i in range(subs): first(0, t, keys, i)

        loop(first_tile, head)
        diag(0)
        for k in range(j_count):
            tot_ref[...] = jnp.zeros((height,128), jnp.float32)
            acc[...] = jnp.zeros_like(acc)
            if k + 1 < j_count:
                begin(k + 1)

                def both(t):
                    keys, vals = tile_of(t, 0), tile_of(t, d)
                    for i in range(subs):
                        first(k + 1, t, keys, i)
                        second(k, t, vals, i)

                loop(first_tile + k + 1, both)
                diag(k + 1)
            else:
                def tail(t):
                    vals = tile_of(t, d)
                    for i in range(subs): second(k, t, vals, i)

                loop(first_tile + k + 1, tail)
            finish(k)

    f32=jnp.float32
    return pl.pallas_call(
        kernel,
        out_shape=jax.ShapeDtypeStruct((j_count, rows, group * d), jnp.bfloat16),
        in_specs=[pl.BlockSpec(memory_space=pltpu.SMEM), pl.BlockSpec(memory_space=pltpu.VMEM)] + [pl.BlockSpec(memory_space=pl.ANY)] * parts_n,
        out_specs=pl.BlockSpec(memory_space=pltpu.VMEM),
        scratch_shapes=[
            pltpu.VMEM((slots * rows, 2 * d), jnp.bfloat16),
            pltpu.VMEM((slots // per_tile, height, tile), f32),
            pltpu.VMEM((slots // per_tile, height, tile), f32),
            pltpu.VMEM((height, 128), f32), pltpu.VMEM((height, 128), f32),
            pltpu.VMEM((height, 128), f32),
            pltpu.VMEM((height, d), f32),
            pltpu.VMEM((height, d), jnp.bfloat16), pltpu.VMEM((height, d), jnp.bfloat16),
            pltpu.SemaphoreType.DMA((parts_n,)),
        ],
        compiler_params=pltpu.CompilerParams(vmem_limit_bytes=26 << 20),
        name="attention",
    )(own, query, *kv_parts)


def build(count):
    bits = count.bit_length() - 1

    def on_device(tokens, gain, w_query, key_value_weight):
        rows = tokens.shape[0]
        d = HEAD_WIDTH
        kv_heads = key_value_weight.shape[1] // (2 * d)
        group = HQ // kv_heads
        j_shift, j_bits = 2, kv_heads.bit_length() - 1
        high = list(range(bits - 1, j_shift + j_bits - 1, -1))
        spread = high + [1, 0]
        own = lax.axis_index("seq")
        own_arr = own.astype(jnp.int32).reshape(1)

        def swap(value, bit):
            return lax.ppermute(value, "seq", [(s, s ^ (1 << bit)) for s in range(count)])

        order = [0]
        for bit in spread:
            order = order + [o | (1 << bit) for o in order]
        j_masks = [r << j_shift for r in range(kv_heads)]
        groups = [[g | m for m in j_masks] for g in range(count) if g & j_masks[-1] == 0]

        def deal(value):
            return lax.all_to_all(value, "seq", 0, 0, axis_index_groups=groups)

        w_all = deal(weights_by_head(w_query, key_value_weight, kv_heads))
        w_all = w_all.reshape(kv_heads * rows, -1)

        def spread_rows(value):
            pieces = [value]
            for bit in spread[:-1]:
                pieces += [swap(p, bit) for p in pieces]
            value = jnp.concatenate(pieces, axis=0)
            return value, swap(value, spread[-1])

        y_bit, z_bit = j_shift, j_shift + 1
        normed = normalize(tokens, gain, own_arr, order, j_shift, kv_heads)
        near, far = normed
        z_near = swap(near, z_bit)
        y_near = swap(near, y_bit)
        y_far = swap(far, y_bit)
        z_far = swap(far, z_bit)
        w_kv = spread_rows(w_all[:, : 2 * d])
        w_q = spread_rows(w_all[:, 2 * d :])
        far_block = (swap(z_near, y_bit), swap(z_far, y_bit))
        blocks = [normed, (y_near, y_far), (z_near, z_far), far_block]

        pairs = [
            [jnp.concatenate([blocks[p][h], blocks[p + 1][h]], axis=0) for h in range(2)]
            for p in range(0, kv_heads, 2)
        ]

        def project(block, w):
            return jnp.dot(block[0], w[0], preferred_element_type=jnp.float32) + jnp.dot(
                block[1], w[1], preferred_element_type=jnp.float32
            )

        half = d // 2
        frequency = ROPE_BASE ** (-(jnp.arange(half, dtype=jnp.float32) * 2.0 / d))

        def table(masks):
            ids = own ^ jnp.array(masks, jnp.int32)
            positions = ids[:, None] * rows + jnp.arange(rows, dtype=jnp.int32)[None, :]
            angles = positions.reshape(-1).astype(jnp.float32)[:, None] * frequency[None, :]
            cosine, sine = jnp.cos(angles), jnp.sin(angles)
            return jnp.concatenate([cosine, cosine], axis=1), jnp.concatenate([-sine, sine], axis=1)

        tables = [table(j_masks[p : p + 2]) for p in range(0, kv_heads, 2)]

        def rotate(u, p):
            cosine, sine = tables[p]
            return u * cosine + jnp.concatenate([u[:, half:], u[:, :half]], axis=1) * sine

        def key_value(p):
            kv = project(pairs[p], w_kv)
            kv = jnp.concatenate([rotate(kv[:, :d], p), kv[:, d:]], axis=1)
            return kv.astype(jnp.bfloat16)

        def query_of(p):
            q = project(pairs[p], w_q)
            return jnp.concatenate(
                [rotate(q[:, h * d : (h + 1) * d], p) for h in range(group)], axis=1
            ).astype(jnp.bfloat16)

        parts = []
        for p in range(2):
            parts += list(spread_rows(key_value(p)))
        query = jnp.concatenate([query_of(p) for p in range(2)], axis=0)
        half_slots = count // 2
        places = [(j_shift, 1), (j_shift + 1, half_slots)]
        places += [(bit, 2 << n) for n, bit in enumerate(spread)]
        dims = (rows, j_shift, kv_heads, group, places)
        out = deal(attention(own_arr, query, parts, dims))
        return out.transpose(1, 0, 2).reshape(rows, HQ * d)

    return on_device


def solution(mesh):
    inner = build(mesh.shape["seq"])

    return jax.shard_map(
        inner,
        mesh=mesh,
        in_specs=(P(("grp", "seq"), None), P(), P("seq", None), P("seq", None)),
        out_specs=P(("grp", "seq"), None),
        check_vma=False,
    )
```

```python
import math

import jax
import jax.numpy as jnp
from jax import lax
from jax.experimental import pallas as pl
from jax.experimental.pallas import tpu as pltpu
from jax.sharding import PartitionSpec as P


HEAD_WIDTH = 128
HQ = 16
ROPE_BASE = 500000.0
NEG = -1e30


def norm_kernel(order, j_shift, j_count, own_ref, tok_ref, gain_ref, *out_refs):
    _, width = tok_ref.shape
    tok = tok_ref[...].astype(jnp.float32)
    mean_sq = jnp.sum(tok * tok, axis=-1, keepdims=True) / width
    inv = lax.rsqrt(mean_sq + 1e-05)
    own = own_ref[0]
    base = own & ~((j_count - 1) << j_shift)
    block = width // (len(order) * j_count)
    places = [(rel, j) for rel in order for j in range(j_count)]
    for n, (rel, j) in enumerate(places):
        source = pl.multiple_of(((base ^ rel) | (j << j_shift)) * block, block)
        piece = tok_ref[:, pl.ds(source, block)].astype(jnp.float32)
        piece = piece * inv * gain_ref[:, pl.ds(source, block)]
        half, place = divmod(n * block, width // 2)
        out_refs[half][:, place : place + block] = piece.astype(jnp.bfloat16)


def normalize(tokens, gain, own, order, j_shift, j_count):
    def kernel(*refs):
        norm_kernel(order, j_shift, j_count, *refs)

    half = jax.ShapeDtypeStruct((tokens.shape[0], tokens.shape[1] // 2), jnp.bfloat16)
    return pl.pallas_call(
        kernel,
        out_shape=(half, half),
        in_specs=[
            pl.BlockSpec(memory_space=pltpu.SMEM),
            pl.BlockSpec(memory_space=pltpu.VMEM),
            pl.BlockSpec(memory_space=pltpu.VMEM),
        ],
        out_specs=(pl.BlockSpec(memory_space=pltpu.VMEM),) * 2,
        compiler_params=pltpu.CompilerParams(vmem_limit_bytes=4 << 20),
        name="norm",
    )(own, tokens, gain.reshape(1, -1))


def weights_by_head(w_query, key_value_weight, heads):
    rows, d = w_query.shape[0], HEAD_WIDTH
    wide = w_query.shape[1] // heads

    def kernel(q_ref, kv_ref, out_ref):
        for j in range(heads):
            out_ref[j, :, :d] = kv_ref[:, j * d : (j + 1) * d]
            out_ref[j, :, d : 2 * d] = kv_ref[:, (heads + j) * d : (heads + j + 1) * d]
            out_ref[j, :, 2 * d :] = q_ref[:, j * wide : (j + 1) * wide]

    return pl.pallas_call(
        kernel,
        out_shape=jax.ShapeDtypeStruct((heads, rows, 2 * d + wide), jnp.bfloat16),
        in_specs=[pl.BlockSpec(memory_space=pltpu.VMEM)] * 2,
        out_specs=pl.BlockSpec(memory_space=pltpu.VMEM),
        name="weights",
    )(w_query, key_value_weight)


def attention(own, query, kv_parts, dims, rels):
    rows, j_shift, group, places, slots = dims
    d = HEAD_WIDTH
    parts_n = len(kv_parts)
    part_rows = kv_parts[0].shape[0]
    whole = parts_n == 1
    per_tile = 1 << j_shift
    tile = per_tile * rows
    height = group * rows
    factor = math.log2(math.e) / math.sqrt(d)
    sub = min(256, height)
    subs = height // sub
    chunks = tile // 128
    last = len(rels) - 1

    def kernel(own_ref, q_ref, *refs):
        part_refs, refs = refs[:parts_n], refs[parts_n:]
        out_refs, refs = refs[: len(rels)], refs[len(rels) :]
        if whole:
            kv = part_refs[0]
        else:
            kv, refs = refs[0], refs[1:]
        scores, tops, queries = refs[0:2], refs[2:4], refs[4:6]
        total_ref, acc, sems = refs[6:9]
        if not whole:
            copies = [
                pltpu.make_async_copy(ref, kv.at[pl.ds(n * part_rows, part_rows)], sems.at[n])
                for n, ref in enumerate(part_refs)
            ]
            for copy in copies:
                copy.start()
        own_id = own_ref[0]
        blocks = [own_id ^ (rel << j_shift) for rel in rels]
        counts = [(block >> j_shift) + 1 for block in blocks]

        def slot_of(block):
            rel = block ^ own_id
            place = 0
            for bit, weight in places:
                place = place + ((rel >> bit) & 1) * weight
            return place

        def tile_of(t, column):
            starts = [
                pl.multiple_of(slot_of(t * per_tile + u) * rows, rows) for u in range(per_tile)
            ]
            return jnp.concatenate([kv[pl.ds(s, rows), column : column + d] for s in starts], axis=0)

        def begin(k):
            q_row = rels[k] * rows
            for h in range(group):
                queries[k % 2][h * rows : (h + 1) * rows] = q_ref[
                    q_row : q_row + rows, h * d : (h + 1) * d
                ]
            tops[k % 2][...] = jnp.full((height, 128), NEG, jnp.float32)

        def first(k, t, keys, i, masked=False):
            r = slice(i * sub, (i + 1) * sub)
            s = lax.dot_general(
                queries[k % 2][r], keys, (((1,), (1,)), ((), ())), preferred_element_type=jnp.float32
            )
            if masked:
                q_row = i * sub + lax.broadcasted_iota(jnp.int32, (sub, tile), 0)
                q_pos = blocks[k] * rows + (q_row & (rows - 1))
                k_pos = t * tile + lax.broadcasted_iota(jnp.int32, (sub, tile), 1)
                s = jnp.where(k_pos <= q_pos, s, NEG)
            scores[k % 2][t, r] = s
            top = tops[k % 2][r]
            for u in range(chunks):
                top = jnp.maximum(top, s[:, u * 128 : (u + 1) * 128])
            tops[k % 2][r] = top

        def second(k, t, vals, i):
            r = slice(i * sub, (i + 1) * sub)
            peak = tops[k % 2][r]
            total = total_ref[r]
            weights = []
            for u in range(chunks):
                s = scores[k % 2][t, r, u * 128 : (u + 1) * 128]
                e = jnp.exp2((s - peak) * factor)
                total = total + e
                weights.append(e.astype(jnp.bfloat16))
            total_ref[r] = total
            acc[r] += jnp.dot(
                jnp.concatenate(weights, axis=1), vals, preferred_element_type=jnp.float32
            )

        def run(start, stop, fresh, done):
            def step(t, carry):
                keys = None if fresh is None else tile_of(t, 0)
                vals = None if done is None else tile_of(t, d)
                for i in range(subs):
                    if fresh is not None:
                        first(fresh, t, keys, i)
                    if done is not None:
                        second(done, t, vals, i)
                return carry

            lax.fori_loop(start, stop, step, 0)

        def diagonal(k):
            t = counts[k] - 1
            keys = tile_of(t, 0)
            for i in range(subs):
                first(k, t, keys, i, True)
            for i in range(subs):
                r = slice(i * sub, (i + 1) * sub)
                peak = jnp.max(tops[k % 2][r], axis=-1, keepdims=True)
                tops[k % 2][r] = jnp.broadcast_to(peak, (sub, 128))

        if not whole:
            for copy in copies:
                copy.wait()
        begin(0)
        run(0, counts[0] - 1, 0, None)
        diagonal(0)
        for k in range(len(rels)):
            total_ref[...] = jnp.zeros((height, 128), jnp.float32)
            acc[...] = jnp.zeros_like(acc)
            if k < last:
                begin(k + 1)
                both = jnp.minimum(counts[k], counts[k + 1] - 1)
                run(0, both, k + 1, k)
                run(both, counts[k], None, k)
                run(both, counts[k + 1] - 1, k + 1, None)
                diagonal(k + 1)
            else:
                run(0, counts[k], None, k)
            for h in range(group):
                r = slice(h * rows, (h + 1) * rows)
                result = acc[r] / jnp.sum(total_ref[r], axis=-1, keepdims=True)
                out_refs[k][:, h * d : (h + 1) * d] = result.astype(jnp.bfloat16)

    f32, bf16 = jnp.float32, jnp.bfloat16
    vmem = pl.BlockSpec(memory_space=pltpu.VMEM)
    outs = [jax.ShapeDtypeStruct((rows, group * d), bf16)] * len(rels)
    if not whole:
        outs.append(jax.ShapeDtypeStruct((slots * rows, 2 * d), bf16))
    kept = min(len(rels), 2)
    score = pltpu.VMEM((slots // per_tile, height, tile), f32)
    small = pltpu.VMEM((8, 128), f32)
    return pl.pallas_call(
        kernel,
        out_shape=outs,
        in_specs=[pl.BlockSpec(memory_space=pltpu.SMEM), vmem]
        + [vmem if whole else pl.BlockSpec(memory_space=pl.ANY)] * parts_n,
        out_specs=[vmem] * len(outs),
        scratch_shapes=[score] * kept
        + [small] * (2 - kept)
        + [pltpu.VMEM((height, 128), f32)] * 2
        + [pltpu.VMEM((height, d), bf16)] * 2
        + [
            pltpu.VMEM((height, 128), f32),
            pltpu.VMEM((height, d), f32),
            pltpu.SemaphoreType.DMA((parts_n,)),
        ],
        compiler_params=pltpu.CompilerParams(vmem_limit_bytes=(10 + 9 * kept) << 20),
        cost_estimate=pl.CostEstimate(
            flops=len(rels) * 2 * slots * rows * height * d,
            bytes_accessed=4 * slots * rows * d,
            transcendentals=len(rels) * slots * rows * height // 2,
        ),
        name="attention",
    )(own, query, *kv_parts)


def place_heads(own, pieces, j_shift):
    count = len(pieces)
    rows, wide = pieces[0].shape

    def kernel(own_ref, *refs):
        own_j = (own_ref[0] >> j_shift) & (count - 1)
        for rel in range(count):
            column = pl.multiple_of((own_j ^ rel) * wide, wide)
            refs[count][:, pl.ds(column, wide)] = refs[rel][...]

    return pl.pallas_call(
        kernel,
        out_shape=jax.ShapeDtypeStruct((rows, count * wide), jnp.bfloat16),
        in_specs=[pl.BlockSpec(memory_space=pltpu.SMEM)]
        + [pl.BlockSpec(memory_space=pltpu.VMEM)] * count,
        out_specs=pl.BlockSpec(memory_space=pltpu.VMEM),
        compiler_params=pltpu.CompilerParams(vmem_limit_bytes=4 << 20),
        name="heads",
    )(own, *pieces)


def build(count):
    bits = count.bit_length() - 1

    def on_device(tokens, gain, w_query, key_value_weight):
        rows = tokens.shape[0]
        d = HEAD_WIDTH
        kv_heads = key_value_weight.shape[1] // (2 * d)
        group = HQ // kv_heads
        j_shift, j_bits = 2, kv_heads.bit_length() - 1
        high = list(range(bits - 1, j_shift + j_bits - 1, -1))
        spread = high + [1, 0]
        own = lax.axis_index("seq")
        own_arr = own.astype(jnp.int32).reshape(1)

        def swap(value, bit):
            return lax.ppermute(value, "seq", [(s, s ^ (1 << bit)) for s in range(count)])

        def exchange(value, mask):
            return lax.ppermute(value, "seq", [(s, s ^ mask) for s in range(count)])

        order = [0]
        for bit in spread:
            order = order + [o | (1 << bit) for o in order]
        j_masks = [r << j_shift for r in range(kv_heads)]
        groups = [[g | m for m in j_masks] for g in range(count) if g & j_masks[-1] == 0]

        def deal(value):
            return lax.all_to_all(value, "seq", 0, 0, axis_index_groups=groups)

        w_all = deal(weights_by_head(w_query, key_value_weight, kv_heads))
        w_all = w_all.reshape(kv_heads * rows, -1)

        def spread_rows(value):
            pieces = [value]
            for bit in spread[:-1]:
                pieces += [swap(p, bit) for p in pieces]
            value = jnp.concatenate(pieces, axis=0)
            return value, swap(value, spread[-1])

        y_bit, z_bit = j_shift, j_shift + 1
        normed = normalize(tokens, gain, own_arr, order, j_shift, kv_heads)
        near, far = normed
        z_near = swap(near, z_bit)
        y_near = swap(near, y_bit)
        y_far = swap(far, y_bit)
        z_far = swap(far, z_bit)
        w_kv = spread_rows(w_all[:, : 2 * d])
        w_q = spread_rows(w_all[:, 2 * d :])
        far_block = (swap(z_near, y_bit), swap(z_far, y_bit))
        blocks = [normed, (y_near, y_far), (z_near, z_far), far_block]

        pairs = [
            [jnp.concatenate([blocks[p][h], blocks[p + 1][h]], axis=0) for h in range(2)]
            for p in range(0, kv_heads, 2)
        ]

        def project(block, w):
            near = jnp.dot(block[0], w[0], preferred_element_type=jnp.float32)
            near = lax.optimization_barrier(near)
            return near + jnp.dot(block[1], w[1], preferred_element_type=jnp.float32)

        half = d // 2
        frequency = ROPE_BASE ** (-(jnp.arange(half, dtype=jnp.float32) * 2.0 / d))

        def table(masks):
            ids = own ^ jnp.array(masks, jnp.int32)
            positions = ids[:, None] * rows + jnp.arange(rows, dtype=jnp.int32)[None, :]
            angles = positions.reshape(-1).astype(jnp.float32)[:, None] * frequency[None, :]
            cosine, sine = jnp.cos(angles), jnp.sin(angles)
            return jnp.concatenate([cosine, cosine], axis=1), jnp.concatenate([-sine, sine], axis=1)

        tables = [table(j_masks[p : p + 2]) for p in range(0, kv_heads, 2)]

        def rotate(u, p):
            cosine, sine = tables[p]
            return u * cosine + jnp.concatenate([u[:, half:], u[:, :half]], axis=1) * sine

        def key_value(p):
            kv = project(pairs[p], w_kv)
            kv = jnp.concatenate([rotate(kv[:, :d], p), kv[:, d:]], axis=1)
            return kv.astype(jnp.bfloat16)

        def query_of(p):
            q = project(pairs[p], w_q)
            return jnp.concatenate(
                [rotate(q[:, h * d : (h + 1) * d], p) for h in range(group)], axis=1
            ).astype(jnp.bfloat16)

        parts = []
        for p in range(2):
            parts += list(spread_rows(key_value(p)))
        query = jnp.concatenate([query_of(p) for p in range(2)], axis=0)
        half_slots = count // 2
        places = [(j_shift, 1), (j_shift + 1, half_slots)]
        places += [(bit, 2 << n) for n, bit in enumerate(spread)]
        dims = (rows, j_shift, group, places, count)
        sent = list(range(kv_heads - 1, 0, -2)) + list(range(2, kv_heads, 2))
        *pieces, kv_all = attention(own_arr, query, parts, dims, sent)
        (own_piece,) = attention(own_arr, query, (kv_all,), dims, [0])
        landed = {0: own_piece}
        for rel, piece in zip(sent, pieces):
            landed[rel] = exchange(piece, rel << j_shift)
        return place_heads(own_arr, [landed[rel] for rel in range(kv_heads)], j_shift)

    return on_device


def solution(mesh):
    inner = build(mesh.shape["seq"])

    return jax.shard_map(
        inner,
        mesh=mesh,
        in_specs=(P(("grp", "seq"), None), P(), P("seq", None), P("seq", None)),
        out_specs=P(("grp", "seq"), None),
        check_vma=False,
    )
```

```python
import math

import jax
import jax.numpy as jnp
from jax import lax
from jax.experimental import pallas as pl
from jax.experimental.pallas import tpu as pltpu
from jax.sharding import PartitionSpec as P


HEAD_WIDTH = 128
HQ = 16
ROPE_BASE = 500000.0
NEG = -1e30


def norm_kernel(order, j_shift, j_count, own_ref, tok_ref, gain_ref, *out_refs):
    _, width = tok_ref.shape
    tok = tok_ref[...].astype(jnp.float32)
    mean_sq = jnp.sum(tok * tok, axis=-1, keepdims=True) / width
    inv = lax.rsqrt(mean_sq + 1e-05)
    own = own_ref[0]
    base = own & ~((j_count - 1) << j_shift)
    block = width // (len(order) * j_count)
    places = [(rel, j) for rel in order for j in range(j_count)]
    for n, (rel, j) in enumerate(places):
        source = pl.multiple_of(((base ^ rel) | (j << j_shift)) * block, block)
        piece = tok_ref[:, pl.ds(source, block)].astype(jnp.float32)
        piece = piece * inv * gain_ref[:, pl.ds(source, block)]
        half, place = divmod(n * block, width // 2)
        out_refs[half][:, place : place + block] = piece.astype(jnp.bfloat16)


def normalize(tokens, gain, own, order, j_shift, j_count):
    def kernel(*refs):
        norm_kernel(order, j_shift, j_count, *refs)

    half = jax.ShapeDtypeStruct((tokens.shape[0], tokens.shape[1] // 2), jnp.bfloat16)
    return pl.pallas_call(
        kernel,
        out_shape=(half, half),
        in_specs=[
            pl.BlockSpec(memory_space=pltpu.SMEM),
            pl.BlockSpec(memory_space=pltpu.VMEM),
            pl.BlockSpec(memory_space=pltpu.VMEM),
        ],
        out_specs=(pl.BlockSpec(memory_space=pltpu.VMEM),) * 2,
        compiler_params=pltpu.CompilerParams(vmem_limit_bytes=4 << 20),
        name="norm",
    )(own, tokens, gain.reshape(1, -1))


def weights_by_head(w_query, key_value_weight, heads):
    rows, d = w_query.shape[0], HEAD_WIDTH
    wide = w_query.shape[1] // heads

    def kernel(q_ref, kv_ref, out_ref, sems):
        copies = []
        for j in range(heads):
            for n, (ref, start, column, size) in enumerate(
                (
                    (kv_ref, j * d, 0, d),
                    (kv_ref, (heads + j) * d, d, d),
                    (q_ref, j * wide, 2 * d, wide),
                )
            ):
                copies.append(
                    pltpu.make_async_copy(
                        ref.at[:, start : start + size],
                        out_ref.at[j, :, column : column + size],
                        sems.at[j, n],
                    )
                )
        for copy in copies:
            copy.start()
        for copy in copies:
            copy.wait()

    return pl.pallas_call(
        kernel,
        out_shape=jax.ShapeDtypeStruct((heads, rows, 2 * d + wide), jnp.bfloat16),
        in_specs=[pl.BlockSpec(memory_space=pl.ANY)] * 2,
        out_specs=pl.BlockSpec(memory_space=pltpu.VMEM),
        scratch_shapes=[pltpu.SemaphoreType.DMA((heads, 3))],
        name="weights",
    )(w_query, key_value_weight)


def attention(own, query, kv_parts, dims, rels):
    rows, j_shift, group, places, slots = dims
    d = HEAD_WIDTH
    parts_n = len(kv_parts)
    part_rows = kv_parts[0].shape[0]
    whole = parts_n == 1
    per_tile = 1 << j_shift
    tile = per_tile * rows
    height = group * rows
    factor = math.log2(math.e) / math.sqrt(d)
    sub = min(512, height)
    subs = height // sub
    chunks = tile // 128
    last = len(rels) - 1

    def kernel(own_ref, q_ref, *refs):
        part_refs, refs = refs[:parts_n], refs[parts_n:]
        out_refs, refs = refs[: len(rels)], refs[len(rels) :]
        if whole:
            kv = part_refs[0]
        else:
            kv, refs = refs[0], refs[1:]
        scores, tops, queries = refs[0:2], refs[2:4], refs[4:6]
        total_ref, acc, sems = refs[6:9]
        if not whole:
            copies = [
                pltpu.make_async_copy(ref, kv.at[pl.ds(n * part_rows, part_rows)], sems.at[n])
                for n, ref in enumerate(part_refs)
            ]
            for copy in copies:
                copy.start()
        own_id = own_ref[0]
        blocks = [own_id ^ (rel << j_shift) for rel in rels]
        counts = [(block >> j_shift) + 1 for block in blocks]

        def slot_of(block):
            rel = block ^ own_id
            place = 0
            for bit, weight in places:
                place = place + ((rel >> bit) & 1) * weight
            return place

        def tile_of(t, column):
            starts = [
                pl.multiple_of(slot_of(t * per_tile + u) * rows, rows) for u in range(per_tile)
            ]
            return jnp.concatenate([kv[pl.ds(s, rows), column : column + d] for s in starts], axis=0)

        def begin(k):
            q_row = rels[k] * rows
            for h in range(group):
                queries[k % 2][h * rows : (h + 1) * rows] = q_ref[
                    q_row : q_row + rows, h * d : (h + 1) * d
                ]
            tops[k % 2][...] = jnp.full((height, 128), NEG, jnp.float32)

        def first(k, t, keys, i, masked=False):
            r = slice(i * sub, (i + 1) * sub)
            s = lax.dot_general(
                queries[k % 2][r], keys, (((1,), (1,)), ((), ())), preferred_element_type=jnp.float32
            )
            if masked:
                q_row = i * sub + lax.broadcasted_iota(jnp.int32, (sub, tile), 0)
                q_pos = blocks[k] * rows + (q_row & (rows - 1))
                k_pos = t * tile + lax.broadcasted_iota(jnp.int32, (sub, tile), 1)
                s = jnp.where(k_pos <= q_pos, s, NEG)
            scores[k % 2][t, r] = s
            top = tops[k % 2][r]
            for u in range(chunks):
                top = jnp.maximum(top, s[:, u * 128 : (u + 1) * 128])
            tops[k % 2][r] = top

        def second(k, t, vals, i):
            r = slice(i * sub, (i + 1) * sub)
            peak = tops[k % 2][r]
            total = total_ref[r]
            weights = []
            for u in range(chunks):
                s = scores[k % 2][t, r, u * 128 : (u + 1) * 128]
                e = jnp.exp2((s - peak) * factor)
                total = total + e
                weights.append(e.astype(jnp.bfloat16))
            total_ref[r] = total
            acc[r] += jnp.dot(
                jnp.concatenate(weights, axis=1), vals, preferred_element_type=jnp.float32
            )

        def run(start, stop, fresh, done):
            def step(t, carry):
                keys = None if fresh is None else tile_of(t, 0)
                vals = None if done is None else tile_of(t, d)
                for i in range(subs):
                    if fresh is not None:
                        first(fresh, t, keys, i)
                    if done is not None:
                        second(done, t, vals, i)
                return carry

            def two_steps(n, carry):
                step(start + 2 * n, carry)
                return step(start + 2 * n + 1, carry)

            pairs = (stop - start) >> 1
            lax.fori_loop(0, pairs, two_steps, 0)
            lax.fori_loop(start + 2 * pairs, stop, step, 0)

        def diagonal(k):
            t = counts[k] - 1
            keys = tile_of(t, 0)
            for i in range(subs):
                first(k, t, keys, i, True)
            for i in range(subs):
                r = slice(i * sub, (i + 1) * sub)
                peak = jnp.max(tops[k % 2][r], axis=-1, keepdims=True)
                tops[k % 2][r] = jnp.broadcast_to(peak, (sub, 128))

        if not whole:
            for copy in copies:
                copy.wait()
        begin(0)
        run(0, counts[0] - 1, 0, None)
        diagonal(0)
        for k in range(len(rels)):
            total_ref[...] = jnp.zeros((height, 128), jnp.float32)
            acc[...] = jnp.zeros_like(acc)
            if k < last:
                begin(k + 1)
                both = jnp.minimum(counts[k], counts[k + 1] - 1)
                run(0, both, k + 1, k)
                run(both, counts[k], None, k)
                run(both, counts[k + 1] - 1, k + 1, None)
                diagonal(k + 1)
            else:
                run(0, counts[k], None, k)
            for h in range(group):
                r = slice(h * rows, (h + 1) * rows)
                result = acc[r] / jnp.sum(total_ref[r], axis=-1, keepdims=True)
                out_refs[k][:, h * d : (h + 1) * d] = result.astype(jnp.bfloat16)

    f32, bf16 = jnp.float32, jnp.bfloat16
    vmem = pl.BlockSpec(memory_space=pltpu.VMEM)
    outs = [jax.ShapeDtypeStruct((rows, group * d), bf16)] * len(rels)
    if not whole:
        outs.append(jax.ShapeDtypeStruct((slots * rows, 2 * d), bf16))
    kept = min(len(rels), 2)
    score = pltpu.VMEM((slots // per_tile, height, tile), f32)
    small = pltpu.VMEM((8, 128), f32)
    return pl.pallas_call(
        kernel,
        out_shape=outs,
        in_specs=[pl.BlockSpec(memory_space=pltpu.SMEM), vmem]
        + [vmem if whole else pl.BlockSpec(memory_space=pl.ANY)] * parts_n,
        out_specs=[vmem] * len(outs),
        scratch_shapes=[score] * kept
        + [small] * (2 - kept)
        + [pltpu.VMEM((height, 128), f32)] * 2
        + [pltpu.VMEM((height, d), bf16)] * 2
        + [
            pltpu.VMEM((height, 128), f32),
            pltpu.VMEM((height, d), f32),
            pltpu.SemaphoreType.DMA((parts_n,)),
        ],
        compiler_params=pltpu.CompilerParams(vmem_limit_bytes=(10 + 9 * kept) << 20),
        cost_estimate=pl.CostEstimate(
            flops=len(rels) * 2 * slots * rows * height * d,
            bytes_accessed=4 * slots * rows * d,
            transcendentals=len(rels) * slots * rows * height // 2,
        ),
        name="attention",
    )(own, query, *kv_parts)


def place_heads(own, pieces, j_shift):
    count = len(pieces)
    rows, wide = pieces[0].shape

    def kernel(own_ref, *refs):
        own_j = (own_ref[0] >> j_shift) & (count - 1)
        for rel in range(count):
            column = pl.multiple_of((own_j ^ rel) * wide, wide)
            refs[count][:, pl.ds(column, wide)] = refs[rel][...]

    return pl.pallas_call(
        kernel,
        out_shape=jax.ShapeDtypeStruct((rows, count * wide), jnp.bfloat16),
        in_specs=[pl.BlockSpec(memory_space=pltpu.SMEM)]
        + [pl.BlockSpec(memory_space=pltpu.VMEM)] * count,
        out_specs=pl.BlockSpec(memory_space=pltpu.VMEM),
        compiler_params=pltpu.CompilerParams(vmem_limit_bytes=4 << 20),
        name="heads",
    )(own, *pieces)


def build(count):
    bits = count.bit_length() - 1

    def on_device(tokens, gain, w_query, key_value_weight):
        rows = tokens.shape[0]
        d = HEAD_WIDTH
        kv_heads = key_value_weight.shape[1] // (2 * d)
        group = HQ // kv_heads
        j_shift, j_bits = 2, kv_heads.bit_length() - 1
        high = list(range(bits - 1, j_shift + j_bits - 1, -1))
        spread = high + [1, 0]
        own = lax.axis_index("seq")
        own_arr = own.astype(jnp.int32).reshape(1)

        def swap(value, bit):
            return lax.ppermute(value, "seq", [(s, s ^ (1 << bit)) for s in range(count)])

        def exchange(value, mask):
            return lax.ppermute(value, "seq", [(s, s ^ mask) for s in range(count)])

        order = [0]
        for bit in spread:
            order = order + [o | (1 << bit) for o in order]
        j_masks = [r << j_shift for r in range(kv_heads)]
        groups = [[g | m for m in j_masks] for g in range(count) if g & j_masks[-1] == 0]

        def deal(value):
            return lax.all_to_all(value, "seq", 0, 0, axis_index_groups=groups)

        w_all = deal(weights_by_head(w_query, key_value_weight, kv_heads))
        w_all = w_all.reshape(kv_heads * rows, -1)

        def spread_rows(value):
            pieces = [value]
            for bit in spread[:-1]:
                pieces += [swap(p, bit) for p in pieces]
            value = jnp.concatenate(pieces, axis=0)
            return value, swap(value, spread[-1])

        y_bit, z_bit = j_shift, j_shift + 1
        normed = normalize(tokens, gain, own_arr, order, j_shift, kv_heads)
        near, far = normed
        z_near = swap(near, z_bit)
        y_near = swap(near, y_bit)
        y_far = swap(far, y_bit)
        z_far = swap(far, z_bit)
        w_kv = spread_rows(w_all[:, : 2 * d])
        w_q = spread_rows(w_all[:, 2 * d :])
        far_block = (swap(z_near, y_bit), swap(z_far, y_bit))
        blocks = [normed, (y_near, y_far), (z_near, z_far), far_block]

        pairs = [
            [jnp.concatenate([blocks[p][h], blocks[p + 1][h]], axis=0) for h in range(2)]
            for p in range(0, kv_heads, 2)
        ]

        def project(block, w):
            near = jnp.dot(block[0], w[0], preferred_element_type=jnp.float32)
            near = lax.optimization_barrier(near)
            return near + jnp.dot(block[1], w[1], preferred_element_type=jnp.float32)

        half = d // 2
        frequency = ROPE_BASE ** (-(jnp.arange(half, dtype=jnp.float32) * 2.0 / d))

        def table(masks):
            ids = own ^ jnp.array(masks, jnp.int32)
            positions = ids[:, None] * rows + jnp.arange(rows, dtype=jnp.int32)[None, :]
            angles = positions.reshape(-1).astype(jnp.float32)[:, None] * frequency[None, :]
            cosine, sine = jnp.cos(angles), jnp.sin(angles)
            return jnp.concatenate([cosine, cosine], axis=1), jnp.concatenate([-sine, sine], axis=1)

        tables = [table(j_masks[p : p + 2]) for p in range(0, kv_heads, 2)]

        def rotate(u, p):
            cosine, sine = tables[p]
            return u * cosine + jnp.concatenate([u[:, half:], u[:, :half]], axis=1) * sine

        def key_value(p):
            kv = project(pairs[p], w_kv)
            kv = jnp.concatenate([rotate(kv[:, :d], p), kv[:, d:]], axis=1)
            return kv.astype(jnp.bfloat16)

        def query_of(p):
            q = project(pairs[p], w_q)
            return jnp.concatenate(
                [rotate(q[:, h * d : (h + 1) * d], p) for h in range(group)], axis=1
            ).astype(jnp.bfloat16)

        parts = []
        for p in range(2):
            parts += list(spread_rows(key_value(p)))
        query = jnp.concatenate([query_of(p) for p in range(2)], axis=0)
        half_slots = count // 2
        places = [(j_shift, 1), (j_shift + 1, half_slots)]
        places += [(bit, 2 << n) for n, bit in enumerate(spread)]
        dims = (rows, j_shift, group, places, count)
        sent = list(range(kv_heads - 1, 0, -2)) + list(range(2, kv_heads, 2))
        *pieces, kv_all = attention(own_arr, query, parts, dims, sent)
        (own_piece,) = attention(own_arr, query, (kv_all,), dims, [0])
        landed = {0: own_piece}
        for rel, piece in zip(sent, pieces):
            landed[rel] = exchange(piece, rel << j_shift)
        return place_heads(own_arr, [landed[rel] for rel in range(kv_heads)], j_shift)

    return on_device


def solution(mesh):
    inner = build(mesh.shape["seq"])

    return jax.shard_map(
        inner,
        mesh=mesh,
        in_specs=(P(("grp", "seq"), None), P(), P("seq", None), P("seq", None)),
        out_specs=P(("grp", "seq"), None),
        check_vma=False,
    )
```

```python
import math

import jax
import jax.numpy as jnp
from jax import lax
from jax.experimental import pallas as pl
from jax.experimental.pallas import tpu as pltpu
from jax.sharding import PartitionSpec as P


HEAD_WIDTH = 128
HQ = 16
ROPE_BASE = 500000.0
NEG = -1e30


def norm_kernel(order, j_shift, j_count, own_ref, tok_ref, gain_ref, *out_refs):
    _, width = tok_ref.shape
    tok = tok_ref[...].astype(jnp.float32)
    mean_sq = jnp.sum(tok * tok, axis=-1, keepdims=True) / width
    inv = lax.rsqrt(mean_sq + 1e-05)
    own = own_ref[0]
    base = own & ~((j_count - 1) << j_shift)
    block = width // (len(order) * j_count)
    places = [(rel, j) for rel in order for j in range(j_count)]
    for n, (rel, j) in enumerate(places):
        source = pl.multiple_of(((base ^ rel) | (j << j_shift)) * block, block)
        piece = tok_ref[:, pl.ds(source, block)].astype(jnp.float32)
        piece = piece * inv * gain_ref[:, pl.ds(source, block)]
        half, place = divmod(n * block, width // 2)
        out_refs[half][:, place : place + block] = piece.astype(jnp.bfloat16)


def normalize(tokens, gain, own, order, j_shift, j_count):
    def kernel(*refs):
        norm_kernel(order, j_shift, j_count, *refs)

    half = jax.ShapeDtypeStruct((tokens.shape[0], tokens.shape[1] // 2), jnp.bfloat16)
    return pl.pallas_call(
        kernel,
        out_shape=(half, half),
        in_specs=[
            pl.BlockSpec(memory_space=pltpu.SMEM),
            pl.BlockSpec(memory_space=pltpu.VMEM),
            pl.BlockSpec(memory_space=pltpu.VMEM),
        ],
        out_specs=(pl.BlockSpec(memory_space=pltpu.VMEM),) * 2,
        compiler_params=pltpu.CompilerParams(vmem_limit_bytes=4 << 20),
        name="norm",
    )(own, tokens, gain.reshape(1, -1))


def weights_by_head(w_query, key_value_weight, heads):
    rows, d = w_query.shape[0], HEAD_WIDTH
    wide = w_query.shape[1] // heads

    def kernel(q_ref, kv_ref, out_ref, sems):
        copies = []
        for j in range(heads):
            for n, (ref, start, column, size) in enumerate(
                (
                    (kv_ref, j * d, 0, d),
                    (kv_ref, (heads + j) * d, d, d),
                    (q_ref, j * wide, 2 * d, wide),
                )
            ):
                copies.append(
                    pltpu.make_async_copy(
                        ref.at[:, start : start + size],
                        out_ref.at[j, :, column : column + size],
                        sems.at[j, n],
                    )
                )
        for copy in copies:
            copy.start()
        for copy in copies:
            copy.wait()

    return pl.pallas_call(
        kernel,
        out_shape=jax.ShapeDtypeStruct((heads, rows, 2 * d + wide), jnp.bfloat16),
        in_specs=[pl.BlockSpec(memory_space=pl.ANY)] * 2,
        out_specs=pl.BlockSpec(memory_space=pltpu.VMEM),
        scratch_shapes=[pltpu.SemaphoreType.DMA((heads, 3))],
        name="weights",
    )(w_query, key_value_weight)


def attention(own, query, kv_parts, dims, rels):
    rows, j_shift, group, places, slots = dims
    d = HEAD_WIDTH
    parts_n = len(kv_parts)
    part_rows = kv_parts[0].shape[0]
    whole = parts_n == 1
    per_tile = 1 << j_shift
    tile = per_tile * rows
    height = group * rows
    factor = math.log2(math.e) / math.sqrt(d)
    sub = min(512, height)
    subs = height // sub
    chunks = tile // 128
    last = len(rels) - 1

    def kernel(own_ref, q_ref, *refs):
        part_refs, refs = refs[:parts_n], refs[parts_n:]
        out_refs, refs = refs[: len(rels)], refs[len(rels) :]
        if whole:
            kv = part_refs[0]
        else:
            kv, refs = refs[0], refs[1:]
        scores, tops, queries = refs[0:2], refs[2:4], refs[4:6]
        total_ref, acc, sems = refs[6:9]
        if not whole:
            copies = [
                pltpu.make_async_copy(ref, kv.at[pl.ds(n * part_rows, part_rows)], sems.at[n])
                for n, ref in enumerate(part_refs)
            ]
            for copy in copies:
                copy.start()
        own_id = own_ref[0]
        blocks = [own_id ^ (rel << j_shift) for rel in rels]
        counts = [(block >> j_shift) + 1 for block in blocks]

        def slot_of(block):
            rel = block ^ own_id
            place = 0
            for bit, weight in places:
                place = place + ((rel >> bit) & 1) * weight
            return place

        def tile_of(t, column):
            starts = [
                pl.multiple_of(slot_of(t * per_tile + u) * rows, rows) for u in range(per_tile)
            ]
            return jnp.concatenate([kv[pl.ds(s, rows), column : column + d] for s in starts], axis=0)

        def begin(k):
            q_row = rels[k] * rows
            for h in range(group):
                queries[k % 2][h * rows : (h + 1) * rows] = q_ref[
                    q_row : q_row + rows, h * d : (h + 1) * d
                ]
            tops[k % 2][...] = jnp.full((height, 128), NEG, jnp.float32)

        def first(k, t, keys, i, masked=False):
            r = slice(i * sub, (i + 1) * sub)
            s = lax.dot_general(
                queries[k % 2][r], keys, (((1,), (1,)), ((), ())), preferred_element_type=jnp.float32
            )
            if masked:
                q_row = i * sub + lax.broadcasted_iota(jnp.int32, (sub, tile), 0)
                q_pos = blocks[k] * rows + (q_row & (rows - 1))
                k_pos = t * tile + lax.broadcasted_iota(jnp.int32, (sub, tile), 1)
                s = jnp.where(k_pos <= q_pos, s, NEG)
            scores[k % 2][t, r] = s
            top = tops[k % 2][r]
            for u in range(chunks):
                top = jnp.maximum(top, s[:, u * 128 : (u + 1) * 128])
            tops[k % 2][r] = top

        def second(k, t, vals, i):
            r = slice(i * sub, (i + 1) * sub)
            peak = tops[k % 2][r]
            total = total_ref[r]
            weights = []
            for u in range(chunks):
                s = scores[k % 2][t, r, u * 128 : (u + 1) * 128]
                e = jnp.exp2((s - peak) * factor)
                total = total + e
                weights.append(e.astype(jnp.bfloat16))
            total_ref[r] = total
            acc[r] += jnp.dot(
                jnp.concatenate(weights, axis=1), vals, preferred_element_type=jnp.float32
            )

        def run(start, stop, fresh, done):
            def step(t, carry):
                keys = None if fresh is None else tile_of(t, 0)
                vals = None if done is None else tile_of(t, d)
                for i in range(subs):
                    if fresh is not None:
                        first(fresh, t, keys, i)
                    if done is not None:
                        second(done, t, vals, i)
                return carry

            def several(size, begin):
                def steps(n, carry):
                    for m in range(size):
                        step(begin + size * n + m, carry)
                    return carry

                return steps

            quads = (stop - start) >> 2
            middle = start + 4 * quads
            pairs = (stop - middle) >> 1
            lax.fori_loop(0, quads, several(4, start), 0)
            lax.fori_loop(0, pairs, several(2, middle), 0)
            lax.fori_loop(middle + 2 * pairs, stop, step, 0)

        def diagonal(k):
            t = counts[k] - 1
            keys = tile_of(t, 0)
            for i in range(subs):
                first(k, t, keys, i, True)
            for i in range(subs):
                r = slice(i * sub, (i + 1) * sub)
                peak = jnp.max(tops[k % 2][r], axis=-1, keepdims=True)
                tops[k % 2][r] = jnp.broadcast_to(peak, (sub, 128))

        if not whole:
            for copy in copies:
                copy.wait()
        begin(0)
        run(0, counts[0] - 1, 0, None)
        diagonal(0)
        for k in range(len(rels)):
            total_ref[...] = jnp.zeros((height, 128), jnp.float32)
            acc[...] = jnp.zeros_like(acc)
            if k < last:
                begin(k + 1)
                both = jnp.minimum(counts[k], counts[k + 1] - 1)
                run(0, both, k + 1, k)
                run(both, counts[k], None, k)
                run(both, counts[k + 1] - 1, k + 1, None)
                diagonal(k + 1)
            else:
                run(0, counts[k], None, k)
            for h in range(group):
                r = slice(h * rows, (h + 1) * rows)
                result = acc[r] / jnp.sum(total_ref[r], axis=-1, keepdims=True)
                out_refs[k][:, h * d : (h + 1) * d] = result.astype(jnp.bfloat16)

    f32, bf16 = jnp.float32, jnp.bfloat16
    vmem = pl.BlockSpec(memory_space=pltpu.VMEM)
    outs = [jax.ShapeDtypeStruct((rows, group * d), bf16)] * len(rels)
    if not whole:
        outs.append(jax.ShapeDtypeStruct((slots * rows, 2 * d), bf16))
    kept = min(len(rels), 2)
    score = pltpu.VMEM((slots // per_tile, height, tile), f32)
    small = pltpu.VMEM((8, 128), f32)
    return pl.pallas_call(
        kernel,
        out_shape=outs,
        in_specs=[pl.BlockSpec(memory_space=pltpu.SMEM), vmem]
        + [vmem if whole else pl.BlockSpec(memory_space=pl.ANY)] * parts_n,
        out_specs=[vmem] * len(outs),
        scratch_shapes=[score] * kept
        + [small] * (2 - kept)
        + [pltpu.VMEM((height, 128), f32)] * 2
        + [pltpu.VMEM((height, d), bf16)] * 2
        + [
            pltpu.VMEM((height, 128), f32),
            pltpu.VMEM((height, d), f32),
            pltpu.SemaphoreType.DMA((parts_n,)),
        ],
        compiler_params=pltpu.CompilerParams(vmem_limit_bytes=(10 + 9 * kept) << 20),
        cost_estimate=pl.CostEstimate(
            flops=len(rels) * 2 * slots * rows * height * d,
            bytes_accessed=4 * slots * rows * d,
            transcendentals=len(rels) * slots * rows * height // 2,
        ),
        name="attention",
    )(own, query, *kv_parts)


def place_heads(own, pieces, j_shift):
    count = len(pieces)
    rows, wide = pieces[0].shape

    def kernel(own_ref, *refs):
        own_j = (own_ref[0] >> j_shift) & (count - 1)
        for rel in range(count):
            column = pl.multiple_of((own_j ^ rel) * wide, wide)
            refs[count][:, pl.ds(column, wide)] = refs[rel][...]

    return pl.pallas_call(
        kernel,
        out_shape=jax.ShapeDtypeStruct((rows, count * wide), jnp.bfloat16),
        in_specs=[pl.BlockSpec(memory_space=pltpu.SMEM)]
        + [pl.BlockSpec(memory_space=pltpu.VMEM)] * count,
        out_specs=pl.BlockSpec(memory_space=pltpu.VMEM),
        compiler_params=pltpu.CompilerParams(vmem_limit_bytes=4 << 20),
        name="heads",
    )(own, *pieces)


def build(count):
    bits = count.bit_length() - 1

    def on_device(tokens, gain, w_query, key_value_weight):
        rows = tokens.shape[0]
        d = HEAD_WIDTH
        kv_heads = key_value_weight.shape[1] // (2 * d)
        group = HQ // kv_heads
        j_shift, j_bits = 2, kv_heads.bit_length() - 1
        high = list(range(bits - 1, j_shift + j_bits - 1, -1))
        spread = high + [1, 0]
        own = lax.axis_index("seq")
        own_arr = own.astype(jnp.int32).reshape(1)

        def swap(value, bit):
            return lax.ppermute(value, "seq", [(s, s ^ (1 << bit)) for s in range(count)])

        def exchange(value, mask):
            return lax.ppermute(value, "seq", [(s, s ^ mask) for s in range(count)])

        order = [0]
        for bit in spread:
            order = order + [o | (1 << bit) for o in order]
        j_masks = [r << j_shift for r in range(kv_heads)]
        groups = [[g | m for m in j_masks] for g in range(count) if g & j_masks[-1] == 0]

        def deal(value):
            return lax.all_to_all(value, "seq", 0, 0, axis_index_groups=groups)

        w_all = deal(weights_by_head(w_query, key_value_weight, kv_heads))
        w_all = w_all.reshape(kv_heads * rows, -1)

        def spread_rows(value):
            pieces = [value]
            for bit in spread[:-1]:
                pieces += [swap(p, bit) for p in pieces]
            value = jnp.concatenate(pieces, axis=0)
            return value, swap(value, spread[-1])

        y_bit, z_bit = j_shift, j_shift + 1
        normed = normalize(tokens, gain, own_arr, order, j_shift, kv_heads)
        near, far = normed
        z_near = swap(near, z_bit)
        y_near = swap(near, y_bit)
        y_far = swap(far, y_bit)
        z_far = swap(far, z_bit)
        w_kv = spread_rows(w_all[:, : 2 * d])
        w_q = spread_rows(w_all[:, 2 * d :])
        far_block = (swap(z_near, y_bit), swap(z_far, y_bit))
        blocks = [normed, (y_near, y_far), (z_near, z_far), far_block]

        pairs = [
            [jnp.concatenate([blocks[p][h], blocks[p + 1][h]], axis=0) for h in range(2)]
            for p in range(0, kv_heads, 2)
        ]

        def project(block, w):
            near = jnp.dot(block[0], w[0], preferred_element_type=jnp.float32)
            near = lax.optimization_barrier(near)
            return near + jnp.dot(block[1], w[1], preferred_element_type=jnp.float32)

        half = d // 2
        frequency = ROPE_BASE ** (-(jnp.arange(half, dtype=jnp.float32) * 2.0 / d))

        def table(masks):
            ids = own ^ jnp.array(masks, jnp.int32)
            positions = ids[:, None] * rows + jnp.arange(rows, dtype=jnp.int32)[None, :]
            angles = positions.reshape(-1).astype(jnp.float32)[:, None] * frequency[None, :]
            cosine, sine = jnp.cos(angles), jnp.sin(angles)
            return jnp.concatenate([cosine, cosine], axis=1), jnp.concatenate([-sine, sine], axis=1)

        tables = [table(j_masks[p : p + 2]) for p in range(0, kv_heads, 2)]

        def rotate(u, p):
            cosine, sine = tables[p]
            return u * cosine + jnp.concatenate([u[:, half:], u[:, :half]], axis=1) * sine

        def key_value(p):
            kv = project(pairs[p], w_kv)
            kv = jnp.concatenate([rotate(kv[:, :d], p), kv[:, d:]], axis=1)
            return kv.astype(jnp.bfloat16)

        def query_of(p):
            q = project(pairs[p], w_q)
            return jnp.concatenate(
                [rotate(q[:, h * d : (h + 1) * d], p) for h in range(group)], axis=1
            ).astype(jnp.bfloat16)

        parts = []
        for p in range(2):
            parts += list(spread_rows(key_value(p)))
        query = jnp.concatenate([query_of(p) for p in range(2)], axis=0)
        half_slots = count // 2
        places = [(j_shift, 1), (j_shift + 1, half_slots)]
        places += [(bit, 2 << n) for n, bit in enumerate(spread)]
        dims = (rows, j_shift, group, places, count)
        sent = list(range(kv_heads - 1, 0, -2)) + list(range(2, kv_heads, 2))
        *pieces, kv_all = attention(own_arr, query, parts, dims, sent[:-1])
        pieces += attention(own_arr, query, (kv_all,), dims, sent[-1:])
        (own_piece,) = attention(own_arr, query, (kv_all,), dims, [0])
        landed = {0: own_piece}
        for rel, piece in zip(sent, pieces):
            landed[rel] = exchange(piece, rel << j_shift)
        return place_heads(own_arr, [landed[rel] for rel in range(kv_heads)], j_shift)

    return on_device


def solution(mesh):
    inner = build(mesh.shape["seq"])

    return jax.shard_map(
        inner,
        mesh=mesh,
        in_specs=(P(("grp", "seq"), None), P(), P("seq", None), P("seq", None)),
        out_specs=P(("grp", "seq"), None),
        check_vma=False,
    )
```

```python
import math

import jax
import jax.numpy as jnp
from jax import lax
from jax.experimental import pallas as pl
from jax.experimental.pallas import tpu as pltpu
from jax.sharding import PartitionSpec as P


HEAD_WIDTH = 128
HQ = 16
ROPE_BASE = 500000.0
NEG = -1e30


def norm_kernel(order, j_shift, j_count, own_ref, tok_ref, gain_ref, *out_refs):
    _, width = tok_ref.shape
    tok = tok_ref[...].astype(jnp.float32)
    mean_sq = jnp.sum(tok * tok, axis=-1, keepdims=True) / width
    inv = lax.rsqrt(mean_sq + 1e-05)
    own = own_ref[0]
    base = own & ~((j_count - 1) << j_shift)
    block = width // (len(order) * j_count)
    places = [(rel, j) for rel in order for j in range(j_count)]
    for n, (rel, j) in enumerate(places):
        source = pl.multiple_of(((base ^ rel) | (j << j_shift)) * block, block)
        piece = tok_ref[:, pl.ds(source, block)].astype(jnp.float32)
        piece = piece * inv * gain_ref[:, pl.ds(source, block)]
        half, place = divmod(n * block, width // 2)
        out_refs[half][:, place : place + block] = piece.astype(jnp.bfloat16)


def normalize(tokens, gain, own, order, j_shift, j_count):
    def kernel(*refs):
        norm_kernel(order, j_shift, j_count, *refs)

    half = jax.ShapeDtypeStruct((tokens.shape[0], tokens.shape[1] // 2), jnp.bfloat16)
    return pl.pallas_call(
        kernel,
        out_shape=(half, half),
        in_specs=[
            pl.BlockSpec(memory_space=pltpu.SMEM),
            pl.BlockSpec(memory_space=pltpu.VMEM),
            pl.BlockSpec(memory_space=pltpu.VMEM),
        ],
        out_specs=(pl.BlockSpec(memory_space=pltpu.VMEM),) * 2,
        compiler_params=pltpu.CompilerParams(vmem_limit_bytes=4 << 20),
        name="norm",
    )(own, tokens, gain.reshape(1, -1))


def weights_by_head(w_query, key_value_weight, heads):
    rows, d = w_query.shape[0], HEAD_WIDTH
    wide = w_query.shape[1] // heads

    def kernel(q_ref, kv_ref, out_ref, sems):
        copies = []
        for j in range(heads):
            for n, (ref, start, column, size) in enumerate(
                (
                    (kv_ref, j * d, 0, d),
                    (kv_ref, (heads + j) * d, d, d),
                    (q_ref, j * wide, 2 * d, wide),
                )
            ):
                copies.append(
                    pltpu.make_async_copy(
                        ref.at[:, start : start + size],
                        out_ref.at[j, :, column : column + size],
                        sems.at[j, n],
                    )
                )
        for copy in copies:
            copy.start()
        for copy in copies:
            copy.wait()

    return pl.pallas_call(
        kernel,
        out_shape=jax.ShapeDtypeStruct((heads, rows, 2 * d + wide), jnp.bfloat16),
        in_specs=[pl.BlockSpec(memory_space=pl.ANY)] * 2,
        out_specs=pl.BlockSpec(memory_space=pltpu.VMEM),
        scratch_shapes=[pltpu.SemaphoreType.DMA((heads, 3))],
        name="weights",
    )(w_query, key_value_weight)


def attention(own, query, kv_parts, dims, rels):
    rows, j_shift, group, places, slots = dims
    d = HEAD_WIDTH
    parts_n = len(kv_parts)
    part_rows = kv_parts[0].shape[0]
    whole = parts_n == 1
    per_tile = 1 << j_shift
    tile = per_tile * rows
    height = group * rows
    factor = math.log2(math.e) / math.sqrt(d)
    sub = min(512, height)
    subs = height // sub
    chunks = tile // 128
    last = len(rels) - 1

    def kernel(own_ref, q_ref, *refs):
        part_refs, refs = refs[:parts_n], refs[parts_n:]
        out_refs, refs = refs[: len(rels)], refs[len(rels) :]
        if whole:
            kv = part_refs[0]
        else:
            kv, refs = refs[0], refs[1:]
        scores, tops, queries = refs[0:2], refs[2:4], refs[4:6]
        total_ref, acc, sems = refs[6:9]
        if not whole:
            copies = [
                pltpu.make_async_copy(ref, kv.at[pl.ds(n * part_rows, part_rows)], sems.at[n])
                for n, ref in enumerate(part_refs)
            ]
            for copy in copies:
                copy.start()
        own_id = own_ref[0]
        blocks = [own_id ^ (rel << j_shift) for rel in rels]
        counts = [(block >> j_shift) + 1 for block in blocks]

        def slot_of(block):
            rel = block ^ own_id
            place = 0
            for bit, weight in places:
                place = place + ((rel >> bit) & 1) * weight
            return place

        def tile_of(t, column):
            starts = [
                pl.multiple_of(slot_of(t * per_tile + u) * rows, rows) for u in range(per_tile)
            ]
            return jnp.concatenate([kv[pl.ds(s, rows), column : column + d] for s in starts], axis=0)

        def begin(k):
            q_row = rels[k] * rows
            for h in range(group):
                queries[k % 2][h * rows : (h + 1) * rows] = q_ref[
                    q_row : q_row + rows, h * d : (h + 1) * d
                ]
            tops[k % 2][...] = jnp.full((height, 128), NEG, jnp.float32)

        def first(k, t, keys, i, masked=False):
            r = slice(i * sub, (i + 1) * sub)
            s = lax.dot_general(
                queries[k % 2][r], keys, (((1,), (1,)), ((), ())), preferred_element_type=jnp.float32
            )
            if masked:
                q_row = i * sub + lax.broadcasted_iota(jnp.int32, (sub, 128), 0)
                ahead = lax.broadcasted_iota(jnp.int32, (sub, 128), 1) - (q_row & (rows - 1))
                room = blocks[k] * rows - t * tile
            top = tops[k % 2][r]
            for u in range(chunks):
                piece = s[:, u * 128 : (u + 1) * 128] * factor
                if masked:
                    piece = jnp.where(ahead <= room - u * 128, piece, NEG)
                scores[k % 2][t, r, u * 128 : (u + 1) * 128] = piece
                top = jnp.maximum(top, piece)
            tops[k % 2][r] = top

        def second(k, t, vals, i):
            r = slice(i * sub, (i + 1) * sub)
            peak = tops[k % 2][r]
            total = total_ref[r]
            weights = []
            for u in range(chunks):
                e = jnp.exp2(scores[k % 2][t, r, u * 128 : (u + 1) * 128] - peak)
                total = total + e
                weights.append(e.astype(jnp.bfloat16))
            total_ref[r] = total
            acc[r] += jnp.dot(
                jnp.concatenate(weights, axis=1), vals, preferred_element_type=jnp.float32
            )

        def run(start, stop, fresh, done):
            def step(t, carry):
                keys = None if fresh is None else tile_of(t, 0)
                vals = None if done is None else tile_of(t, d)
                for i in range(subs):
                    if fresh is not None:
                        first(fresh, t, keys, i)
                    if done is not None:
                        second(done, t, vals, i)
                return carry

            def several(size, begin):
                def steps(n, carry):
                    for m in range(size):
                        step(begin + size * n + m, carry)
                    return carry

                return steps

            quads = (stop - start) >> 2
            middle = start + 4 * quads
            pairs = (stop - middle) >> 1
            lax.fori_loop(0, quads, several(4, start), 0)
            lax.fori_loop(0, pairs, several(2, middle), 0)
            lax.fori_loop(middle + 2 * pairs, stop, step, 0)

        def diagonal(k):
            t = counts[k] - 1
            keys = tile_of(t, 0)
            for i in range(subs):
                first(k, t, keys, i, True)
            for i in range(subs):
                r = slice(i * sub, (i + 1) * sub)
                peak = jnp.max(tops[k % 2][r], axis=-1, keepdims=True)
                tops[k % 2][r] = jnp.broadcast_to(peak, (sub, 128))

        if not whole:
            for copy in copies:
                copy.wait()
        begin(0)
        run(0, counts[0] - 1, 0, None)
        diagonal(0)
        for k in range(len(rels)):
            total_ref[...] = jnp.zeros((height, 128), jnp.float32)
            acc[...] = jnp.zeros_like(acc)
            if k < last:
                begin(k + 1)
                both = jnp.minimum(counts[k], counts[k + 1] - 1)
                run(0, both, k + 1, k)
                run(both, counts[k], None, k)
                run(both, counts[k + 1] - 1, k + 1, None)
                diagonal(k + 1)
            else:
                run(0, counts[k], None, k)
            for h in range(group):
                r = slice(h * rows, (h + 1) * rows)
                result = acc[r] / jnp.sum(total_ref[r], axis=-1, keepdims=True)
                out_refs[k][:, h * d : (h + 1) * d] = result.astype(jnp.bfloat16)

    f32, bf16 = jnp.float32, jnp.bfloat16
    vmem = pl.BlockSpec(memory_space=pltpu.VMEM)
    outs = [jax.ShapeDtypeStruct((rows, group * d), bf16)] * len(rels)
    if not whole:
        outs.append(jax.ShapeDtypeStruct((slots * rows, 2 * d), bf16))
    kept = min(len(rels), 2)
    score = pltpu.VMEM((slots // per_tile, height, tile), f32)
    small = pltpu.VMEM((8, 128), f32)
    return pl.pallas_call(
        kernel,
        out_shape=outs,
        in_specs=[pl.BlockSpec(memory_space=pltpu.SMEM), vmem]
        + [vmem if whole else pl.BlockSpec(memory_space=pl.ANY)] * parts_n,
        out_specs=[vmem] * len(outs),
        scratch_shapes=[score] * kept
        + [small] * (2 - kept)
        + [pltpu.VMEM((height, 128), f32)] * 2
        + [pltpu.VMEM((height, d), bf16)] * 2
        + [
            pltpu.VMEM((height, 128), f32),
            pltpu.VMEM((height, d), f32),
            pltpu.SemaphoreType.DMA((parts_n,)),
        ],
        compiler_params=pltpu.CompilerParams(vmem_limit_bytes=(10 + 9 * kept) << 20),
        cost_estimate=pl.CostEstimate(
            flops=len(rels) * 2 * slots * rows * height * d,
            bytes_accessed=4 * slots * rows * d,
            transcendentals=len(rels) * slots * rows * height // 2,
        ),
        name="attention",
    )(own, query, *kv_parts)


def place_heads(own, pieces, j_shift):
    count = len(pieces)
    rows, wide = pieces[0].shape

    def kernel(own_ref, *refs):
        own_j = (own_ref[0] >> j_shift) & (count - 1)
        for rel in range(count):
            column = pl.multiple_of((own_j ^ rel) * wide, wide)
            refs[count][:, pl.ds(column, wide)] = refs[rel][...]

    return pl.pallas_call(
        kernel,
        out_shape=jax.ShapeDtypeStruct((rows, count * wide), jnp.bfloat16),
        in_specs=[pl.BlockSpec(memory_space=pltpu.SMEM)]
        + [pl.BlockSpec(memory_space=pltpu.VMEM)] * count,
        out_specs=pl.BlockSpec(memory_space=pltpu.VMEM),
        compiler_params=pltpu.CompilerParams(vmem_limit_bytes=4 << 20),
        name="heads",
    )(own, *pieces)


def build(count):
    bits = count.bit_length() - 1

    def on_device(tokens, gain, w_query, key_value_weight):
        rows = tokens.shape[0]
        d = HEAD_WIDTH
        kv_heads = key_value_weight.shape[1] // (2 * d)
        group = HQ // kv_heads
        j_shift, j_bits = 2, kv_heads.bit_length() - 1
        high = list(range(bits - 1, j_shift + j_bits - 1, -1))
        spread = high + [1, 0]
        own = lax.axis_index("seq")
        own_arr = own.astype(jnp.int32).reshape(1)

        def swap(value, bit):
            return lax.ppermute(value, "seq", [(s, s ^ (1 << bit)) for s in range(count)])

        def exchange(value, mask):
            return lax.ppermute(value, "seq", [(s, s ^ mask) for s in range(count)])

        order = [0]
        for bit in spread:
            order = order + [o | (1 << bit) for o in order]
        j_masks = [r << j_shift for r in range(kv_heads)]
        groups = [[g | m for m in j_masks] for g in range(count) if g & j_masks[-1] == 0]

        def deal(value):
            return lax.all_to_all(value, "seq", 0, 0, axis_index_groups=groups)

        w_all = deal(weights_by_head(w_query, key_value_weight, kv_heads))
        w_all = w_all.reshape(kv_heads * rows, -1)

        def spread_rows(value):
            pieces = [value]
            for bit in spread[:-1]:
                pieces += [swap(p, bit) for p in pieces]
            value = jnp.concatenate(pieces, axis=0)
            return value, swap(value, spread[-1])

        y_bit, z_bit = j_shift, j_shift + 1
        normed = normalize(tokens, gain, own_arr, order, j_shift, kv_heads)
        near, far = normed
        z_near = swap(near, z_bit)
        y_near = swap(near, y_bit)
        y_far = swap(far, y_bit)
        z_far = swap(far, z_bit)
        w_kv = spread_rows(w_all[:, : 2 * d])
        w_q = spread_rows(w_all[:, 2 * d :])
        far_block = (swap(z_near, y_bit), swap(z_far, y_bit))
        blocks = [normed, (y_near, y_far), (z_near, z_far), far_block]

        pairs = [
            [jnp.concatenate([blocks[p][h], blocks[p + 1][h]], axis=0) for h in range(2)]
            for p in range(0, kv_heads, 2)
        ]

        def project(block, w):
            near = jnp.dot(block[0], w[0], preferred_element_type=jnp.float32)
            near = lax.optimization_barrier(near)
            return near + jnp.dot(block[1], w[1], preferred_element_type=jnp.float32)

        half = d // 2
        frequency = ROPE_BASE ** (-(jnp.arange(half, dtype=jnp.float32) * 2.0 / d))

        def table(masks):
            ids = own ^ jnp.array(masks, jnp.int32)
            positions = ids[:, None] * rows + jnp.arange(rows, dtype=jnp.int32)[None, :]
            angles = positions.reshape(-1).astype(jnp.float32)[:, None] * frequency[None, :]
            cosine, sine = jnp.cos(angles), jnp.sin(angles)
            return jnp.concatenate([cosine, cosine], axis=1), jnp.concatenate([-sine, sine], axis=1)

        tables = [table(j_masks[p : p + 2]) for p in range(0, kv_heads, 2)]

        def rotate(u, p):
            cosine, sine = tables[p]
            return u * cosine + jnp.concatenate([u[:, half:], u[:, :half]], axis=1) * sine

        def key_value(p):
            kv = project(pairs[p], w_kv)
            kv = jnp.concatenate([rotate(kv[:, :d], p), kv[:, d:]], axis=1)
            return kv.astype(jnp.bfloat16)

        def query_of(p):
            q = project(pairs[p], w_q)
            return jnp.concatenate(
                [rotate(q[:, h * d : (h + 1) * d], p) for h in range(group)], axis=1
            ).astype(jnp.bfloat16)

        parts = []
        for p in range(2):
            parts += list(spread_rows(key_value(p)))
        query = jnp.concatenate([query_of(p) for p in range(2)], axis=0)
        half_slots = count // 2
        places = [(j_shift, 1), (j_shift + 1, half_slots)]
        places += [(bit, 2 << n) for n, bit in enumerate(spread)]
        dims = (rows, j_shift, group, places, count)
        sent = list(range(kv_heads - 1, 0, -2)) + list(range(2, kv_heads, 2))
        *pieces, kv_all = attention(own_arr, query, parts, dims, sent[:-1])
        pieces += attention(own_arr, query, (kv_all,), dims, sent[-1:])
        (own_piece,) = attention(own_arr, query, (kv_all,), dims, [0])
        landed = {0: own_piece}
        for rel, piece in zip(sent, pieces):
            landed[rel] = exchange(piece, rel << j_shift)
        return place_heads(own_arr, [landed[rel] for rel in range(kv_heads)], j_shift)

    return on_device


def solution(mesh):
    inner = build(mesh.shape["seq"])

    return jax.shard_map(
        inner,
        mesh=mesh,
        in_specs=(P(("grp", "seq"), None), P(), P("seq", None), P("seq", None)),
        out_specs=P(("grp", "seq"), None),
        check_vma=False,
    )
```
